32 devices in a mesh: rows: 8 (over z, x), feat: 4 (over y, core).
Axes of the slice: x: 2, y: 2, z: 4, core: 2. Of those that a mesh axis runs over, the one named last changes fastest.
Arguments:
- features: float32 [16384, 1024], P('rows', 'feat')
- norm_gain: float32 [1024], P('feat'), may hold values from 0.1 to 1.9
- row_counts: int32 [8, 16], P('rows'), may hold values from 1 to 43, 86 in all within a row
- tile_cols: int32 [688], P('rows'), may hold values from 0 to 127, as said below
- tile_values: float32 [688, 128, 128], P('rows'), may hold values from -0.1875 to 0.1875
Outputs:
- normed: float32 [16384, 1024], P('rows', 'feat')
The draws below stay inside these ranges and needn't reach their ends.
Inputs may be any that keep to these rules, and one draw needn't show every extreme that they name: `tile_cols`: node n lies in stripe n // 2048. There are exactly 3 heavy stripes; every device's tiles reference every block of every heavy stripe and every block of its own stripe. Every other block that a device's tiles reference is referenced by one of its tiles only, lies in no heavy stripe, and no two such blocks of one device lie in the same stripe; each device has exactly 3 such blocks. `row_counts`: each device's counts sum to 86.
All inputs are finite; a program needn't handle non-finite values.
Results may differ from the reference program's by a relative error of at most 0.0003.
Values sent between devices are 32-bit elements; how exact they have to be, the bound alone decides.
No kernel may reach another device: no remote copies, remote signals or barrier semaphores. Data moves between devices by JAX's collectives and lax.ppermute only.
A program may use at most 128 MiB of HBM per device.

```python
import math
import jax
import jax.numpy as jnp
import numpy as np
from jax import lax

F = 1024
NODE_DEV = 2048
BLOCK = 128
HEAVY = 3
SPARE = 19
BLK_DEV = 16
NODES = 16384
NEED = 3
TILES = 86
MOST = 43
N_ROWS = 8


def shuffle_row(row_key, row_ids):
    return jax.random.permutation(row_key, row_ids)


def owner_ranking(row_key):
    return jax.random.permutation(row_key, N_ROWS)


def build_plan(key):
    base_key = jax.random.fold_in(key, 4242)
    key_heavy, key_rank, key_block, key_spare, key_shuffle = jax.random.split(base_key, 5)
    owner_order = jax.random.permutation(key_heavy, N_ROWS)
    heavy_devs = owner_order[:HEAVY].astype(jnp.int32)
    owner_ids = jnp.arange(N_ROWS, dtype=jnp.int32)
    reader_ids = owner_ids[:, None]
    owner_heavy = jnp.any(owner_ids[:, None] == heavy_devs[None, :], axis=1)
    rank_table = jax.vmap(owner_ranking)(jax.random.split(key_rank, N_ROWS)).astype(jnp.int32)
    blocked = owner_heavy[None, :] | (owner_ids[None, :] == reader_ids)
    scores = rank_table + N_ROWS * blocked.astype(jnp.int32)
    chosen = jnp.argsort(scores, axis=1, stable=True)[:, :NEED].astype(jnp.int32)
    picked = jax.random.randint(key_block, (N_ROWS, NEED), 0, BLK_DEV, dtype=jnp.int32)
    light_ids = chosen * BLK_DEV + picked
    block_ids = jnp.arange(BLK_DEV, dtype=jnp.int32)
    heavy_list = (heavy_devs[:, None] * BLK_DEV + block_ids[None, :]).reshape(-1)
    own_list = reader_ids * BLK_DEV + block_ids[None, :]
    pool_ids = jnp.concatenate([jnp.broadcast_to(heavy_list[None, :], (N_ROWS, HEAVY * BLK_DEV)), own_list], axis=1)
    extra_pick = jax.random.randint(key_spare, (N_ROWS, SPARE), 0, (HEAVY + 1) * BLK_DEV, dtype=jnp.int32)
    extra_ids = jnp.take_along_axis(pool_ids, extra_pick, axis=1)
    every_id = jnp.concatenate([light_ids, pool_ids, extra_ids], axis=1)
    shuffled = jax.vmap(shuffle_row)(jax.random.split(key_shuffle, N_ROWS), every_id)
    return shuffled.astype(jnp.int32)


def draw_tile_cols(key, part):
    shuffled = build_plan(key)
    return shuffled.reshape(-1)


def draw_features(key, part):
    key_val, key_col = jax.random.split(jax.random.fold_in(key, 77), 2)
    ramp_values = jnp.arange(F, dtype=jnp.float32) / F
    col_scale = 10.0 ** (0.5 * ramp_values + 0.5 * jax.random.uniform(key_col, (F,), jnp.float32))
    values = jnp.clip(jax.random.normal(key_val, (NODES, F), jnp.float32), -5.0, 5.0)
    return values * col_scale[None, :]


def level_of(stream_key, dims, cuts, least, high):
    factor_of = 1.0
    for axis_at, shards_of in cuts:
        heights = jax.random.uniform(jax.random.fold_in(jax.random.fold_in(stream_key, 6), axis_at), (shards_of,), jnp.float32, least / len(cuts), high / len(cuts))
        factor_of = factor_of * jnp.repeat(jnp.exp(heights), dims[axis_at] // shards_of).reshape((-1,) + (1,) * (len(dims) - 1 - axis_at))
    return factor_of


def length_profile(amount, total, bound, lean):
    loads = [(1 << 20) // math.isqrt(rank ** lean) + 1 for rank in range(2, amount + 1)]
    surplus, counts = total - bound - (amount - 1), [1] * (amount - 1)
    while surplus > 0:
        free = [i for i in range(amount - 1) if counts[i] < bound]
        mass, remaining = sum([loads[i] for i in free]), surplus
        for i in free:
            addition = min(bound - counts[i], max(1, remaining * loads[i] // mass), surplus)
            counts[i] = counts[i] + addition
            surplus = surplus - addition
    return np.array([bound] + counts)


def uneven_parts(key, amount, total, bound, skew):
    if amount == 2:
        one = jax.random.randint(key, (), max(1, total - bound), min(bound, total - 1) + 1)
        return jnp.stack([one, total - one])
    tallies = jnp.asarray(length_profile(amount, total, bound, skew), jnp.int32)
    pairs = (amount - 1) // 2
    giver, receiver = tallies[1:1 + 2 * pairs:2], tallies[2:2 + 2 * pairs:2]
    room = jnp.minimum(giver - 1, bound - receiver)
    passed = jax.random.randint(jax.random.fold_in(key, 1), (pairs,), 0, 1 << 20) % (room + 1)
    tallies = tallies.at[1:1 + 2 * pairs:2].set(giver - passed).at[2:2 + 2 * pairs:2].set(receiver + passed)
    return tallies[jax.random.permutation(jax.random.fold_in(key, 2), amount)]


def bell_draw(own_key, extent, width, most, cuts=(), kind=jnp.bfloat16):
    level = level_of(own_key, extent, cuts, -0.22, 0.18) if cuts else 1.0
    array = jax.random.normal(own_key, extent, jnp.float32) * width * level
    return jnp.minimum(jnp.maximum(array, -most), most).astype(kind)


def setup_inputs(seed: int = 0) -> dict:
    key_of = jax.random.split(jax.random.key(seed), 6)
    return {
        "features": draw_features(jax.random.fold_in(key_of[5], 71), 0),
        "norm_gain": jnp.clip(1.0 + 0.18 * jax.random.normal(key_of[1], (F,), jnp.float32), 0.1, 1.9),
        "row_counts": jax.vmap(lambda own: uneven_parts(own, BLK_DEV, TILES, MOST, 2))(jax.random.split(key_of[2], N_ROWS)).reshape((N_ROWS, BLK_DEV)).astype(jnp.int32),
        "tile_cols": draw_tile_cols(jax.random.fold_in(key_of[5], 71), 0),
        "tile_values": bell_draw(key_of[4], (N_ROWS * TILES, BLOCK, BLOCK), (BLOCK * 8) ** -0.5, 0.1875, ((0, 8),), jnp.float32),
    }


def reference(features, norm_gain, row_counts, tile_cols, tile_values):
    activated = jnp.maximum(features, 0.0)
    act_blocks = activated.reshape(NODES // BLOCK, BLOCK, F)
    tile_index = jnp.arange(TILES, dtype=jnp.int32)
    row_ids = jnp.arange(BLK_DEV, dtype=jnp.int32)

    def one_device(device):
        tile_counts = lax.dynamic_index_in_dim(row_counts, device, 0, keepdims=False)
        row_ends = jnp.cumsum(tile_counts, dtype=jnp.int32)
        tile_row = lax.optimization_barrier(jnp.sum((row_ends[None, :] <= tile_index[:, None]).astype(jnp.int32), axis=1))
        onehot = (tile_row[None, :] == row_ids[:, None]).astype(jnp.float32)
        block_cols = lax.dynamic_slice_in_dim(tile_cols, (device * TILES).astype(jnp.int32), TILES)
        tile_vals = lax.dynamic_slice_in_dim(tile_values, (device * TILES).astype(jnp.int32), TILES)
        picked = act_blocks[block_cols]
        products = jnp.einsum('tij,tjf->tif', tile_vals, picked, precision=lax.Precision.HIGHEST)
        summed = jnp.dot(onehot, products.reshape(TILES, BLOCK * F), precision=lax.Precision.HIGHEST, preferred_element_type=jnp.float32)
        return summed.reshape(NODE_DEV, F)
    aggregate = lax.map(one_device, jnp.arange(N_ROWS, dtype=jnp.int32)).reshape(NODES, F)
    mean_square = lax.optimization_barrier(jnp.mean(aggregate * aggregate, axis=1, keepdims=True))
    return aggregate * norm_gain[None, :] * lax.rsqrt(mean_square + 1e-05)
```

```python
import functools

import jax
import jax.numpy as jnp
from jax import lax
from jax.experimental import pallas as pl
from jax.experimental.pallas import tpu as pltpu
from jax.sharding import PartitionSpec as P


HEAVY = 3
SMEM = pl.BlockSpec(memory_space=pltpu.SMEM)
VMEM = pl.BlockSpec(memory_space=pltpu.VMEM)


def ring_order(n):
    return list(range(0, n, 2)) + list(range(n - 1, 0, -2))


def ring_place(index, n):
    return jnp.where(index % 2 == 0, index // 2, n - 1 - index // 2)


def wants_kernel(n, blocks_dev, tile_total, cols_ref, want_ref, heavy_ref, mine_ref, seen_ref):
    me = lax.axis_index("rows")

    @pl.loop(0, n)
    def _(o):
        seen_ref[o] = 0

        @pl.loop(0, n)
        def _(p):
            want_ref[o, p] = 0

    @pl.loop(0, tile_total)
    def _(t):
        col = cols_ref[t]
        owner = col // blocks_dev
        seen_ref[owner] = seen_ref[owner] + 1
        want_ref[me, owner] = col % blocks_dev

    def count(o, found):
        return found + ((seen_ref[o] >= 2) & (o != me)).astype(jnp.int32)

    others = lax.fori_loop(0, n, count, 0)
    mine = (others < HEAVY).astype(jnp.int32)
    mine_ref[0] = mine
    for k in range(HEAVY):
        heavy_ref[k] = 0

    def rank(o, found):
        is_heavy = ((seen_ref[o] >= 2) & (o != me)) | ((o == me) & (mine == 1))

        @pl.when(is_heavy)
        def _():
            heavy_ref[jnp.minimum(found, HEAVY - 1)] = o

        return found + is_heavy.astype(jnp.int32)

    lax.fori_loop(0, n, rank, 0)


def find_wants(n, blocks_dev, tile_cols):
    tile_total = tile_cols.shape[0]
    return pl.pallas_call(
        functools.partial(wants_kernel, n, blocks_dev, tile_total),
        out_shape=(
            jax.ShapeDtypeStruct((n, n), jnp.int32),
            jax.ShapeDtypeStruct((HEAVY,), jnp.int32),
            jax.ShapeDtypeStruct((1,), jnp.int32),
        ),
        in_specs=[SMEM],
        out_specs=(SMEM, SMEM, SMEM),
        scratch_shapes=[pltpu.SMEM((n,), jnp.int32)],
        name="wants",
    )(tile_cols)


def order_kernel(
    n, blocks_dev, tile_total, lists, ring, cols_ref, counts_ref, heavy_ref, plan_ref, list_ref, code_ref
):
    me = lax.axis_index("rows")
    here = ring_place(me, n)
    slots = max(n, blocks_dev * (1 if ring else HEAVY))

    @pl.loop(0, lists)
    def _(g):
        plan_ref[g] = 0

    def row_body(j, t0):
        def tile_body(t, carry):
            col = cols_ref[t]
            owner = col // blocks_dev
            local = col % blocks_dev
            heavy_at = jnp.int32(-1)
            for k in range(HEAVY):
                heavy_at = jnp.where(owner == heavy_ref[k], k, heavy_at)
            if ring:
                half = local // n
                there = ring_place(local % n, n)
                hops = jnp.where(half == 0, here - there, there - here)
                hops = jnp.where(hops < 0, hops + n, hops)
                single = (half == 1) & (hops == n - 1) & (heavy_at == HEAVY - 1)
                heavy_list = 2 + 2 * hops + half + single.astype(jnp.int32)
                heavy_slot = jnp.where(single, 0, heavy_at)
            else:
                heavy_list, heavy_slot = 2, heavy_at * blocks_dev + local
            own = owner == me
            which = jnp.where(own, 0, jnp.where(heavy_at < 0, 1, heavy_list))
            slot = jnp.where(own, local, jnp.where(heavy_at < 0, owner, heavy_slot))
            list_ref[t] = which
            plan_ref[which] = plan_ref[which] + 1
            code_ref[t] = (t * blocks_dev + j) * slots + slot
            return carry

        stop = jnp.minimum(t0 + counts_ref[0, j], tile_total)
        lax.fori_loop(t0, stop, tile_body, 0)
        return stop

    lax.fori_loop(0, counts_ref.shape[1], row_body, 0)

    def add_up(g, total):
        count = plan_ref[g]
        plan_ref[g] = total
        return total + count

    lax.fori_loop(0, lists, add_up, 0)

    @pl.loop(0, tile_total)
    def _(t):
        which = list_ref[t]
        at = plan_ref[which]
        plan_ref[which] = at + 1
        plan_ref[lists + at] = code_ref[t]


def order_tiles(n, blocks_dev, lists, ring, tile_cols, row_counts, heavy_ids):
    tile_total = tile_cols.shape[0]
    return pl.pallas_call(
        functools.partial(order_kernel, n, blocks_dev, tile_total, lists, ring),
        out_shape=jax.ShapeDtypeStruct((lists + tile_total,), jnp.int32),
        in_specs=[SMEM] * 3,
        out_specs=SMEM,
        scratch_shapes=[pltpu.SMEM((tile_total,), jnp.int32), pltpu.SMEM((tile_total,), jnp.int32)],
        name="order",
    )(tile_cols, row_counts, heavy_ids)


def pick_kernel(choose, count, *refs):
    index_refs, from_ref, out_ref, sem_ref = refs[:-3], refs[-3], refs[-2], refs[-1]
    copies = [
        pltpu.make_async_copy(from_ref.at[choose(k, *index_refs)], out_ref.at[k], sem_ref.at[k])
        for k in range(count)
    ]
    for copy in copies:
        copy.start()
    for copy in copies:
        copy.wait()


def pick_blocks(choose, count, indices, blocks, to):
    return pl.pallas_call(
        functools.partial(pick_kernel, choose, count),
        out_shape=jax.ShapeDtypeStruct((count, *blocks.shape[1:]), blocks.dtype),
        in_specs=[SMEM] * len(indices) + [VMEM],
        out_specs=pl.BlockSpec(memory_space=to),
        scratch_shapes=[pltpu.SemaphoreType.DMA((count,))],
        compiler_params=pltpu.CompilerParams(vmem_limit_bytes=8 << 20),
        cost_estimate=pl.CostEstimate(
            flops=0, bytes_accessed=8 * count * blocks.shape[1] * blocks.shape[2], transcendentals=0
        ),
        name="pick",
    )(*indices, blocks)


def halves(x):
    high = x.astype(jnp.bfloat16)
    low = (x - high.astype(jnp.float32)).astype(jnp.bfloat16)
    return high, low


def add_kernel(lists, all_lists, slots, first, plan_ref, tiles_ref, *refs):
    panels, out_ref = refs[: len(lists)], refs[-1]
    blocks_dev = out_ref.shape[0]
    if first:
        out_ref[...] = jnp.zeros_like(out_ref)
    for which, panel in zip(lists, panels):
        begin = plan_ref[which - 1] if which else 0

        @pl.loop(begin, plan_ref[which])
        def _(i):
            code = plan_ref[all_lists + i]
            at, slot = code // slots, code % slots
            tile, row = at // blocks_dev, at % blocks_dev
            a_high, a_low = halves(tiles_ref[tile])
            x_high, x_low = halves(jnp.maximum(panel[slot], 0.0))
            left = jnp.concatenate([a_high, a_low, a_high], axis=1)
            right = jnp.concatenate([x_high, x_high, x_low], axis=0)
            out_ref[row] += jnp.dot(left, right, preferred_element_type=jnp.float32)


def add_products(plan, tiles, lists, panels, into, blocks_dev, slots):
    tile_total, block, _ = tiles.shape
    width = panels[0].shape[-1]
    first = into is None
    operands = [plan, tiles, *panels] + ([] if first else [into])
    return pl.pallas_call(
        functools.partial(add_kernel, lists, plan.shape[0] - tile_total, slots, first),
        out_shape=jax.ShapeDtypeStruct((blocks_dev, block, width), jnp.float32),
        in_specs=[SMEM] + [VMEM] * (len(operands) - 1),
        out_specs=VMEM,
        input_output_aliases={} if first else {len(operands) - 1: 0},
        compiler_params=pltpu.CompilerParams(vmem_limit_bytes=24 << 20),
        cost_estimate=pl.CostEstimate(
            flops=20 * len(lists) * block * block * width,
            bytes_accessed=4 * blocks_dev * block * width,
            transcendentals=0,
        ),
        name="add",
    )(*operands)


def per_device(features, norm_gain, row_counts, tile_cols, tile_values):
    node_dev, width = features.shape
    _, block, _ = tile_values.shape
    blocks_dev = node_dev // block
    n = lax.axis_size("rows")
    ring = blocks_dev == 2 * n and n & (n - 1) == 0
    slots = max(n, blocks_dev * (1 if ring else HEAVY))
    blocks = features.reshape(blocks_dev, block, width)
    swap = functools.partial(lax.all_to_all, axis_name="rows", split_axis=0, concat_axis=0, tiled=True)
    tie = lax.optimization_barrier
    if ring:
        lists = 3 + 2 * n
        source, tile_cols = tie((blocks[:n], tile_cols))
        first_part = swap(source)
        want, heavy_ids, mine = find_wants(n, blocks_dev, tile_cols)
        want = lax.psum(want, "rows")

        def second_block(k, want, mine):
            asked = jnp.clip(want[k, lax.axis_index("rows")], 0, blocks_dev - 1)
            return jnp.where(mine[0] == 1, n + k, asked)

        picked = pick_blocks(second_block, n, (want, mine), blocks, pltpu.HBM)
        first_part, picked = tie((first_part, picked))
        second_part = swap(picked)
        order = ring_order(n)
        up = [(order[i], order[(i + 1) % n]) for i in range(n)]
        down = [(b, a) for a, b in up]
        share = functools.partial(pick_blocks, lambda k, ids: ids[k], HEAVY, (heavy_ids,), to=pltpu.VMEM)
        start = share(first_part)
        start, row_counts = tie((start, row_counts))
        plan = order_tiles(n, blocks_dev, lists, True, tile_cols, row_counts, heavy_ids)
        add = functools.partial(add_products, plan, tile_values, blocks_dev=blocks_dev, slots=slots)
        ahead = lax.ppermute(start, "rows", up)
        total = add((0, 2), (blocks, start), None)
        second_part, total = tie((second_part, total))
        mine_back = share(second_part)
        back = mine_back
        ready = [(1, second_part), (3, back), (4, ahead)]
        for hop in range(1, n - 1):
            back = lax.ppermute(back, "rows", down)
            ahead = lax.ppermute(ahead, "rows", up)
            total = add(tuple(g for g, _ in ready), tuple(p for _, p in ready), total)
            ahead, total = tie((ahead, total))
            ready = [(3 + 2 * hop, back), (4 + 2 * hop, ahead)]
        third = HEAVY - 1
        back = lax.ppermute(back[third:], "rows", down)
        straight = lax.ppermute(mine_back[:third], "rows", up)
        total = add(tuple(g for g, _ in ready), tuple(p for _, p in ready), total)
        straight, total = tie((straight, total))
        total = add((2 * n + 1, 2 * n + 2), (straight, back), total)
    else:
        want, heavy_ids, mine = find_wants(n, blocks_dev, tile_cols)
        me = lax.axis_index("rows")
        asked = swap(want[me].reshape(n, 1))[:, 0]
        plan = order_tiles(n, blocks_dev, 3, False, tile_cols, row_counts, heavy_ids)
        piece = node_dev // n
        light = swap(blocks[asked])
        scattered = swap(features.reshape(n, piece, width))[heavy_ids]
        heavy = lax.all_gather(scattered, "rows", axis=1, tiled=True).reshape(HEAVY * blocks_dev, block, width)
        total = add_products(plan, tile_values, (0, 1, 2), (blocks, light, heavy), None, blocks_dev, slots)
    aggregate = total.reshape(node_dev, width)
    square_sum = jnp.sum(lax.all_gather(jnp.sum(aggregate * aggregate, axis=1), "feat"), axis=0)
    mean_square = square_sum / (width * lax.axis_size("feat"))
    return aggregate * norm_gain[None, :] * lax.rsqrt(mean_square + 1e-05)[:, None]


def solution(mesh):
    placed = (P("rows", "feat"), P("feat"), P("rows", None), P("rows"), P("rows", None, None))
    return jax.shard_map(per_device, mesh=mesh, in_specs=placed, out_specs=P("rows", "feat"), check_vma=False)
```

```python
import functools

import jax
import jax.numpy as jnp
from jax import lax
from jax.experimental import pallas as pl
from jax.experimental.pallas import tpu as pltpu
from jax.sharding import PartitionSpec as P


HEAVY = 3
SMEM = pl.BlockSpec(memory_space=pltpu.SMEM)
HBM = pl.BlockSpec(memory_space=pltpu.HBM)
VMEM = pl.BlockSpec(memory_space=pltpu.VMEM)


def ring_order(n):
    return list(range(0, n, 2)) + list(range(n - 1, 0, -2))


def ring_place(index, n):
    return jnp.where(index % 2 == 0, index // 2, n - 1 - index // 2)


def find_heavy(n, blocks_dev, tile_total, cols_ref, heavy_ref, mine_ref, seen_ref, last_ref):
    me = lax.axis_index("rows")

    @pl.loop(0, n)
    def _(o):
        seen_ref[o] = 0
        last_ref[o] = 0

    @pl.loop(0, tile_total)
    def _(t):
        col = cols_ref[t]
        owner = col // blocks_dev
        seen_ref[owner] = seen_ref[owner] + 1
        last_ref[owner] = col % blocks_dev

    for k in range(HEAVY):
        heavy_ref[k] = 0

    def count(o, found):
        return found + ((seen_ref[o] >= 2) & (o != me)).astype(jnp.int32)

    others = lax.fori_loop(0, n, count, 0)
    mine = (others < HEAVY).astype(jnp.int32)
    mine_ref[0] = mine

    def rank(o, found):
        is_heavy = ((seen_ref[o] >= 2) & (o != me)) | ((o == me) & (mine == 1))

        @pl.when(is_heavy)
        def _():
            heavy_ref[jnp.minimum(found, HEAVY - 1)] = o

        return found + is_heavy.astype(jnp.int32)

    lax.fori_loop(0, n, rank, 0)


def wants_kernel(n, blocks_dev, tile_total, cols_ref, heavy_ref, mine_ref, want_ref, seen_ref):
    find_heavy(n, blocks_dev, tile_total, cols_ref, heavy_ref, mine_ref, seen_ref, want_ref)


def find_wants(n, blocks_dev, tile_cols):
    tile_total = tile_cols.shape[0]
    ints = lambda count: jax.ShapeDtypeStruct((count,), jnp.int32)
    return pl.pallas_call(
        functools.partial(wants_kernel, n, blocks_dev, tile_total),
        out_shape=(ints(HEAVY), ints(1), ints(n)),
        in_specs=[SMEM],
        out_specs=(SMEM,) * 3,
        scratch_shapes=[pltpu.SMEM((n,), jnp.int32)],
        name="wants",
    )(tile_cols)


def head_kernel(
    n, blocks_dev, tile_total, cols_ref, from_ref,
    heavy_ref, mine_ref, want_ref, half_ref,
    seen_ref, last_ref, buf_ref, in_sem, out_sem,
):
    ins = [pltpu.make_async_copy(from_ref.at[k], buf_ref.at[k], in_sem.at[k]) for k in range(n)]
    outs = [pltpu.make_async_copy(buf_ref.at[k], half_ref.at[k], out_sem.at[k]) for k in range(n)]
    for copy in ins:
        copy.start()
    me = lax.axis_index("rows")
    for o in range(n):
        for p in range(n):
            want_ref[o, p] = 0
    for copy, onward in zip(ins, outs):
        copy.wait()
        onward.start()
    find_heavy(n, blocks_dev, tile_total, cols_ref, heavy_ref, mine_ref, seen_ref, last_ref)
    for p in range(n):
        want_ref[me, p] = last_ref[p]
    for copy in outs:
        copy.wait()


def start_up(n, blocks_dev, tile_cols, blocks):
    tile_total = tile_cols.shape[0]
    shape = (n, *blocks.shape[1:])
    return pl.pallas_call(
        functools.partial(head_kernel, n, blocks_dev, tile_total),
        out_shape=(
            jax.ShapeDtypeStruct((HEAVY,), jnp.int32),
            jax.ShapeDtypeStruct((1,), jnp.int32),
            jax.ShapeDtypeStruct((n, n), jnp.int32),
            pltpu.HBM(shape, jnp.float32),
        ),
        in_specs=[SMEM, HBM],
        out_specs=(SMEM, SMEM, SMEM, HBM),
        scratch_shapes=[
            pltpu.SMEM((n,), jnp.int32),
            pltpu.SMEM((n,), jnp.int32),
            pltpu.VMEM(shape, jnp.float32),
            pltpu.SemaphoreType.DMA((n,)),
            pltpu.SemaphoreType.DMA((n,)),
        ],
        name="head",
    )(tile_cols, blocks)


def order_kernel(
    n, blocks_dev, tile_total, lists, ring, cols_ref, counts_ref, heavy_ref, plan_ref, list_ref, code_ref
):
    me = lax.axis_index("rows")
    here = ring_place(me, n)
    slots = max(n, blocks_dev * (1 if ring else HEAVY))

    @pl.loop(0, lists)
    def _(g):
        plan_ref[g] = 0

    def row_body(j, t0):
        def tile_body(t, carry):
            col = cols_ref[t]
            owner = col // blocks_dev
            local = col % blocks_dev
            heavy_at = jnp.int32(-1)
            for k in range(HEAVY):
                heavy_at = jnp.where(owner == heavy_ref[k], k, heavy_at)
            if ring:
                half = local // n
                there = ring_place(local % n, n)
                hops = jnp.where(half == 0, here - there, there - here)
                hops = jnp.where(hops < 0, hops + n, hops)
                heavy_list, heavy_slot = 2 + 2 * hops + half, heavy_at
            else:
                heavy_list, heavy_slot = 2, heavy_at * blocks_dev + local
            own = owner == me
            which = jnp.where(own, 0, jnp.where(heavy_at < 0, 1, heavy_list))
            slot = jnp.where(own, local, jnp.where(heavy_at < 0, owner, heavy_slot))
            list_ref[t] = which
            plan_ref[which] = plan_ref[which] + 1
            code_ref[t] = (t * blocks_dev + j) * slots + slot
            return carry

        stop = jnp.minimum(t0 + counts_ref[0, j], tile_total)
        lax.fori_loop(t0, stop, tile_body, 0)
        return stop

    lax.fori_loop(0, counts_ref.shape[1], row_body, 0)

    def add_up(g, total):
        count = plan_ref[g]
        plan_ref[g] = total
        return total + count

    lax.fori_loop(0, lists, add_up, 0)

    @pl.loop(0, tile_total)
    def _(t):
        which = list_ref[t]
        at = plan_ref[which]
        plan_ref[which] = at + 1
        plan_ref[lists + at] = code_ref[t]


def order_tiles(n, blocks_dev, lists, ring, tile_cols, row_counts, heavy_ids):
    tile_total = tile_cols.shape[0]
    return pl.pallas_call(
        functools.partial(order_kernel, n, blocks_dev, tile_total, lists, ring),
        out_shape=jax.ShapeDtypeStruct((lists + tile_total,), jnp.int32),
        in_specs=[SMEM] * 3,
        out_specs=SMEM,
        scratch_shapes=[pltpu.SMEM((tile_total,), jnp.int32), pltpu.SMEM((tile_total,), jnp.int32)],
        name="order",
    )(tile_cols, row_counts, heavy_ids)


def pick_kernel(choose, count, *refs):
    index_refs, from_ref, out_ref, sem_ref = refs[:-3], refs[-3], refs[-2], refs[-1]
    copies = [
        pltpu.make_async_copy(from_ref.at[choose(k, *index_refs)], out_ref.at[k], sem_ref.at[k])
        for k in range(count)
    ]
    for copy in copies:
        copy.start()
    for copy in copies:
        copy.wait()


def pick_blocks(choose, count, indices, blocks, at, to):
    return pl.pallas_call(
        functools.partial(pick_kernel, choose, count),
        out_shape=to((count, *blocks.shape[1:]), blocks.dtype),
        in_specs=[SMEM] * len(indices) + [pl.BlockSpec(memory_space=at)],
        out_specs=pl.BlockSpec(memory_space=to),
        scratch_shapes=[pltpu.SemaphoreType.DMA((count,))],
        compiler_params=pltpu.CompilerParams(vmem_limit_bytes=8 << 20),
        cost_estimate=pl.CostEstimate(
            flops=0, bytes_accessed=8 * count * blocks.shape[1] * blocks.shape[2], transcendentals=0
        ),
        name="pick",
    )(*indices, blocks)


def halves(x):
    high = x.astype(jnp.bfloat16)
    low = (x - high.astype(jnp.float32)).astype(jnp.bfloat16)
    return high, low


def add_kernel(lists, all_lists, slots, first, plan_ref, tiles_ref, *refs):
    panels = refs[: len(lists)]
    if first:
        out_ref, kept_ref, sem_ref = refs[len(lists):]
        bring = pltpu.make_async_copy(tiles_ref, kept_ref, sem_ref)
        bring.start()
        out_ref[...] = jnp.zeros_like(out_ref)
        bring.wait()
        tiles_ref = kept_ref
    else:
        out_ref = refs[-1]
    blocks_dev = out_ref.shape[0]
    for which, panel in zip(lists, panels):
        begin = plan_ref[which - 1] if which else 0

        @pl.loop(begin, plan_ref[which])
        def _(i):
            code = plan_ref[all_lists + i]
            at, slot = code // slots, code % slots
            tile, row = at // blocks_dev, at % blocks_dev
            a_high, a_low = halves(tiles_ref[tile])
            x_high, x_low = halves(jnp.maximum(panel[slot], 0.0))
            left = jnp.concatenate([a_high, a_low, a_high], axis=1)
            right = jnp.concatenate([x_high, x_high, x_low], axis=0)
            out_ref[row] += jnp.dot(left, right, preferred_element_type=jnp.float32)


def add_products(plan, tiles, lists, panels, into, blocks_dev, slots):
    tile_total, block, _ = tiles.shape
    width = panels[0].shape[-1]
    first = into is None
    operands = [plan, tiles, *panels] + ([] if first else [into])
    total = pltpu.VMEM((blocks_dev, block, width), jnp.float32)
    done = pl.pallas_call(
        functools.partial(add_kernel, lists, plan.shape[0] - tile_total, slots, first),
        out_shape=(total, pltpu.VMEM(tiles.shape, tiles.dtype)) if first else total,
        in_specs=[SMEM, HBM if first else VMEM] + [VMEM] * (len(operands) - 2),
        out_specs=(VMEM, VMEM) if first else VMEM,
        scratch_shapes=[pltpu.SemaphoreType.DMA] if first else [],
        input_output_aliases={} if first else {len(operands) - 1: 0},
        compiler_params=pltpu.CompilerParams(vmem_limit_bytes=16 << 20),
        cost_estimate=pl.CostEstimate(
            flops=20 * len(lists) * block * block * width,
            bytes_accessed=4 * blocks_dev * block * width,
            transcendentals=0,
        ),
        name="add",
    )(*operands)
    return done if first else (done, tiles)


def per_device(features, norm_gain, row_counts, tile_cols, tile_values):
    node_dev, width = features.shape
    _, block, _ = tile_values.shape
    blocks_dev = node_dev // block
    n = lax.axis_size("rows")
    ring = blocks_dev == 2 * n and n & (n - 1) == 0
    slots = max(n, blocks_dev * (1 if ring else HEAVY))
    blocks = features.reshape(blocks_dev, block, width)
    swap = functools.partial(lax.all_to_all, axis_name="rows", split_axis=0, concat_axis=0, tiled=True)
    tie = lax.optimization_barrier
    if ring:
        lists = 2 + 2 * n
        heavy_ids, mine, want, source = start_up(n, blocks_dev, tile_cols, blocks)
        first_part = swap(source)
        flip = lambda x, m: lax.ppermute(x, "rows", [(i, i ^ m) for i in range(n)])
        want = [want, flip(want, 1)]
        pair = want[0] + want[1]
        want = [pair] + [flip(pair, m) for m in range(2, n, 2)]

        def second_block(k, mine, *want):
            me = lax.axis_index("rows")
            asked = sum(matrix[k, me] for matrix in want)
            return jnp.where(mine[0] == 1, n + k, jnp.clip(asked, 0, blocks_dev - 1))

        picked = pick_blocks(second_block, n, (mine, *want), blocks, pltpu.VMEM, pltpu.HBM)
        second_part = swap(picked)
        order = ring_order(n)
        up = [(order[i], order[(i + 1) % n]) for i in range(n)]
        down = [(b, a) for a, b in up]
        share = functools.partial(pick_blocks, lambda k, ids: ids[k], HEAVY, (heavy_ids,), at=pl.ANY, to=pltpu.VMEM)
        start = share(first_part)
        start, row_counts = tie((start, row_counts))
        plan = order_tiles(n, blocks_dev, lists, True, tile_cols, row_counts, heavy_ids)
        add = functools.partial(add_products, plan, blocks_dev=blocks_dev, slots=slots)

        def hop_on(way, x):
            return lax.ppermute(x, "rows", up if way == "up" else down)

        def add_now(ready, tiles, total):
            lists, panels = zip(*ready)
            total, tiles = add(tiles, lists, panels, total)
            return tiles, total

        ahead = hop_on("up", start)
        straight = hop_on("down", start)
        sums = add_now([(0, blocks), (2, start)], tile_values, None)
        sums = add_now([(4, ahead), (2 * n, straight)], *sums)
        back = mine_back = share(second_part)
        ready = [(1, second_part), (3, back)]
        ahead = hop_on("up", ahead)
        for hop in range(1, n - 1):
            if hop < n - 2:
                ready.append((4 + 2 * hop, ahead))
            else:
                ready.append((2 * n + 1, ahead))
            if hop < n - 3:
                ahead = hop_on("up", ahead)
            elif hop == n - 3:
                mine_back, ahead = tie((mine_back, ahead))
                ahead = hop_on("up", mine_back)
            back = hop_on("down", back)
            sums = add_now(ready, *sums)
            ready = [(3 + 2 * hop, back)]
        _, total = add_now(ready, *sums)
    else:
        heavy_ids, _, want = find_wants(n, blocks_dev, tile_cols)
        asked = swap(want.reshape(n, 1))[:, 0]
        plan = order_tiles(n, blocks_dev, 3, False, tile_cols, row_counts, heavy_ids)
        piece = node_dev // n
        light = swap(blocks[asked])
        scattered = swap(features.reshape(n, piece, width))[heavy_ids]
        heavy = lax.all_gather(scattered, "rows", axis=1, tiled=True).reshape(HEAVY * blocks_dev, block, width)
        total, _ = add_products(plan, tile_values, (0, 1, 2), (blocks, light, heavy), None, blocks_dev, slots)
    aggregate = total.reshape(node_dev, width)
    square_sum = jnp.sum(lax.all_gather(jnp.sum(aggregate * aggregate, axis=1), "feat"), axis=0)
    mean_square = square_sum / (width * lax.axis_size("feat"))
    return aggregate * norm_gain[None, :] * lax.rsqrt(mean_square + 1e-05)[:, None]


def solution(mesh):
    placed = (P("rows", "feat"), P("feat"), P("rows", None), P("rows"), P("rows", None, None))
    return jax.shard_map(per_device, mesh=mesh, in_specs=placed, out_specs=P("rows", "feat"), check_vma=False)
```

```python
import functools

import jax
import jax.numpy as jnp
from jax import lax
from jax.experimental import pallas as pl
from jax.experimental.pallas import tpu as pltpu
from jax.sharding import PartitionSpec as P


HEAVY = 3
SMEM = pl.BlockSpec(memory_space=pltpu.SMEM)
HBM = pl.BlockSpec(memory_space=pltpu.HBM)
ANY = pl.BlockSpec(memory_space=pl.ANY)
VMEM = pl.BlockSpec(memory_space=pltpu.VMEM)


def ring_order(n):
    return list(range(0, n, 2)) + list(range(n - 1, 0, -2))


def ring_place(index, n):
    return jnp.where(index % 2 == 0, index // 2, n - 1 - index // 2)


def find_heavy(n, blocks_dev, tile_total, cols_ref, heavy_ref, mine_ref, seen_ref, last_ref):
    me = lax.axis_index("rows")

    @pl.loop(0, n)
    def _(o):
        seen_ref[o] = 0
        last_ref[o] = 0

    @pl.loop(0, tile_total)
    def _(t):
        col = cols_ref[t]
        owner = col // blocks_dev
        seen_ref[owner] = seen_ref[owner] + 1
        last_ref[owner] = col % blocks_dev

    for k in range(HEAVY):
        heavy_ref[k] = 0

    def count(o, found):
        return found + ((seen_ref[o] >= 2) & (o != me)).astype(jnp.int32)

    others = lax.fori_loop(0, n, count, 0)
    mine = (others < HEAVY).astype(jnp.int32)
    mine_ref[0] = mine

    def rank(o, found):
        is_heavy = ((seen_ref[o] >= 2) & (o != me)) | ((o == me) & (mine == 1))

        @pl.when(is_heavy)
        def _():
            heavy_ref[jnp.minimum(found, HEAVY - 1)] = o

        return found + is_heavy.astype(jnp.int32)

    lax.fori_loop(0, n, rank, 0)


def wants_kernel(n, blocks_dev, tile_total, cols_ref, heavy_ref, mine_ref, want_ref, seen_ref):
    find_heavy(n, blocks_dev, tile_total, cols_ref, heavy_ref, mine_ref, seen_ref, want_ref)


def find_wants(n, blocks_dev, tile_cols):
    tile_total = tile_cols.shape[0]
    ints = lambda count: jax.ShapeDtypeStruct((count,), jnp.int32)
    return pl.pallas_call(
        functools.partial(wants_kernel, n, blocks_dev, tile_total),
        out_shape=(ints(HEAVY), ints(1), ints(n)),
        in_specs=[SMEM],
        out_specs=(SMEM,) * 3,
        scratch_shapes=[pltpu.SMEM((n,), jnp.int32)],
        name="wants",
    )(tile_cols)


def head_kernel(n, blocks_dev, tile_total, cols_ref, from_ref, heavy_ref, mine_ref, want_ref, *refs):
    letters, (seen_ref, last_ref, sem_ref) = refs[: n - 1], refs[n - 1:]
    copies = [pltpu.make_async_copy(from_ref.at[m], letters[m - 1], sem_ref.at[m - 1]) for m in range(1, n)]
    for copy in copies:
        copy.start()
    me = lax.axis_index("rows")
    for o in range(n):
        for p in range(n):
            want_ref[o, p] = 0
    find_heavy(n, blocks_dev, tile_total, cols_ref, heavy_ref, mine_ref, seen_ref, last_ref)
    for p in range(n):
        want_ref[me, p] = last_ref[p]
    for copy in copies:
        copy.wait()


def start_up(n, blocks_dev, tile_cols, blocks):
    tile_total = tile_cols.shape[0]
    letter = pltpu.VMEM(blocks.shape[1:], jnp.float32)
    heavy_ids, mine, want, *letters = pl.pallas_call(
        functools.partial(head_kernel, n, blocks_dev, tile_total),
        out_shape=(
            jax.ShapeDtypeStruct((HEAVY,), jnp.int32),
            jax.ShapeDtypeStruct((1,), jnp.int32),
            jax.ShapeDtypeStruct((n, n), jnp.int32),
            *[letter] * (n - 1),
        ),
        in_specs=[SMEM, HBM],
        out_specs=(SMEM, SMEM, SMEM, *[VMEM] * (n - 1)),
        scratch_shapes=[
            pltpu.SMEM((n,), jnp.int32),
            pltpu.SMEM((n,), jnp.int32),
            pltpu.SemaphoreType.DMA((n - 1,)),
        ],
        compiler_params=pltpu.CompilerParams(vmem_limit_bytes=58 << 20),
        name="head",
    )(tile_cols, pltpu.with_memory_space_constraint(blocks, pltpu.HBM))
    return heavy_ids, mine, want, letters


def share_kernel(n, home, heavy_ref, from_ref, *refs):
    got, (out_ref, sem_ref) = refs[: n - 1], refs[n - 1:]
    me = lax.axis_index("rows")
    for k in range(HEAVY):
        away = heavy_ref[k] ^ me
        for m in range(n):
            source = from_ref.at[home] if m == 0 else got[m - 1]

            @pl.when(away == m)
            def _(source=source, k=k):
                pltpu.make_async_copy(source, out_ref.at[k], sem_ref.at[k]).start()

    for k in range(HEAVY):
        pltpu.make_async_copy(from_ref.at[home], out_ref.at[k], sem_ref.at[k]).wait()


def take_share(n, home, heavy_ids, blocks, got):
    _, block, width = blocks.shape
    return pl.pallas_call(
        functools.partial(share_kernel, n, home),
        out_shape=jax.ShapeDtypeStruct((HEAVY, block, width), jnp.float32),
        in_specs=[SMEM, ANY] + [ANY] * (n - 1),
        out_specs=VMEM,
        scratch_shapes=[pltpu.SemaphoreType.DMA((HEAVY,))],
        compiler_params=pltpu.CompilerParams(vmem_limit_bytes=8 << 20),
        cost_estimate=pl.CostEstimate(flops=0, bytes_accessed=8 * HEAVY * block * width, transcendentals=0),
        name="share",
    )(heavy_ids, blocks, *got)


def order_kernel(
    n, blocks_dev, tile_total, lists, ring, cols_ref, counts_ref, heavy_ref, plan_ref, list_ref, code_ref
):
    me = lax.axis_index("rows")
    here = ring_place(me, n)
    slots = max(n, blocks_dev * (1 if ring else HEAVY))

    @pl.loop(0, lists)
    def _(g):
        plan_ref[g] = 0

    def row_body(j, t0):
        def tile_body(t, carry):
            col = cols_ref[t]
            owner = col // blocks_dev
            local = col % blocks_dev
            heavy_at = jnp.int32(-1)
            for k in range(HEAVY):
                heavy_at = jnp.where(owner == heavy_ref[k], k, heavy_at)
            if ring:
                half = local // n
                there = ring_place(jnp.where(half == 0, owner ^ (local % n), local % n), n)
                hops = jnp.where(half == 0, here - there, there - here)
                hops = jnp.where(hops < 0, hops + n, hops)
                heavy_list, heavy_slot = 2 + 2 * hops + half, heavy_at
            else:
                heavy_list, heavy_slot = 2, heavy_at * blocks_dev + local
            own = owner == me
            which = jnp.where(own, 0, jnp.where(heavy_at < 0, 1, heavy_list))
            slot = jnp.where(own, local, jnp.where(heavy_at < 0, owner, heavy_slot))
            list_ref[t] = which
            plan_ref[which] = plan_ref[which] + 1
            code_ref[t] = (t * blocks_dev + j) * slots + slot
            return carry

        stop = jnp.minimum(t0 + counts_ref[0, j], tile_total)
        lax.fori_loop(t0, stop, tile_body, 0)
        return stop

    lax.fori_loop(0, counts_ref.shape[1], row_body, 0)

    def add_up(g, total):
        count = plan_ref[g]
        plan_ref[g] = total
        return total + count

    lax.fori_loop(0, lists, add_up, 0)

    @pl.loop(0, tile_total)
    def _(t):
        which = list_ref[t]
        at = plan_ref[which]
        plan_ref[which] = at + 1
        plan_ref[lists + at] = code_ref[t]


def order_tiles(n, blocks_dev, lists, ring, tile_cols, row_counts, heavy_ids):
    tile_total = tile_cols.shape[0]
    return pl.pallas_call(
        functools.partial(order_kernel, n, blocks_dev, tile_total, lists, ring),
        out_shape=jax.ShapeDtypeStruct((lists + tile_total,), jnp.int32),
        in_specs=[SMEM] * 3,
        out_specs=SMEM,
        scratch_shapes=[pltpu.SMEM((tile_total,), jnp.int32), pltpu.SMEM((tile_total,), jnp.int32)],
        name="order",
    )(tile_cols, row_counts, heavy_ids)


def pick_kernel(choose, count, *refs):
    index_refs, from_ref, out_ref, sem_ref = refs[:-3], refs[-3], refs[-2], refs[-1]
    copies = [
        pltpu.make_async_copy(from_ref.at[choose(k, *index_refs)], out_ref.at[k], sem_ref.at[k])
        for k in range(count)
    ]
    for copy in copies:
        copy.start()
    for copy in copies:
        copy.wait()


def pick_blocks(choose, count, indices, blocks, at, to):
    return pl.pallas_call(
        functools.partial(pick_kernel, choose, count),
        out_shape=to((count, *blocks.shape[1:]), blocks.dtype),
        in_specs=[SMEM] * len(indices) + [pl.BlockSpec(memory_space=at)],
        out_specs=pl.BlockSpec(memory_space=to),
        scratch_shapes=[pltpu.SemaphoreType.DMA((count,))],
        compiler_params=pltpu.CompilerParams(vmem_limit_bytes=8 << 20),
        cost_estimate=pl.CostEstimate(
            flops=0, bytes_accessed=8 * count * blocks.shape[1] * blocks.shape[2], transcendentals=0
        ),
        name="pick",
    )(*indices, blocks)


def halves(x):
    high = x.astype(jnp.bfloat16)
    low = (x - high.astype(jnp.float32)).astype(jnp.bfloat16)
    return high, low


def add_kernel(lists, all_lists, slots, first, plan_ref, tiles_ref, *refs):
    panels = refs[: len(lists)]
    if first:
        out_ref, kept_ref, sem_ref = refs[len(lists):]
        bring = pltpu.make_async_copy(tiles_ref, kept_ref, sem_ref)
        bring.start()
        out_ref[...] = jnp.zeros_like(out_ref)
        bring.wait()
        tiles_ref = kept_ref
    else:
        out_ref = refs[-1]
    blocks_dev = out_ref.shape[0]
    for which, panel in zip(lists, panels):
        begin = plan_ref[which - 1] if which else 0

        @pl.loop(begin, plan_ref[which])
        def _(i):
            code = plan_ref[all_lists + i]
            at, slot = code // slots, code % slots
            tile, row = at // blocks_dev, at % blocks_dev
            a_high, a_low = halves(tiles_ref[tile])
            x_high, x_low = halves(jnp.maximum(panel[slot], 0.0))
            left = jnp.concatenate([a_high, a_low, a_high], axis=1)
            right = jnp.concatenate([x_high, x_high, x_low], axis=0)
            out_ref[row] += jnp.dot(left, right, preferred_element_type=jnp.float32)


def add_products(plan, tiles, lists, panels, into, blocks_dev, slots):
    tile_total, block, _ = tiles.shape
    width = panels[0].shape[-1]
    first = into is None
    operands = [plan, tiles, *panels] + ([] if first else [into])
    total = pltpu.VMEM((blocks_dev, block, width), jnp.float32)
    done = pl.pallas_call(
        functools.partial(add_kernel, lists, plan.shape[0] - tile_total, slots, first),
        out_shape=(total, pltpu.VMEM(tiles.shape, tiles.dtype)) if first else total,
        in_specs=[SMEM, HBM if first else VMEM] + [VMEM] * (len(operands) - 2),
        out_specs=(VMEM, VMEM) if first else VMEM,
        scratch_shapes=[pltpu.SemaphoreType.DMA] if first else [],
        input_output_aliases={} if first else {len(operands) - 1: 0},
        compiler_params=pltpu.CompilerParams(vmem_limit_bytes=16 << 20),
        cost_estimate=pl.CostEstimate(
            flops=20 * len(lists) * block * block * width,
            bytes_accessed=4 * blocks_dev * block * width,
            transcendentals=0,
        ),
        name="add",
    )(*operands)
    return done if first else (done, tiles)


def per_device(features, norm_gain, row_counts, tile_cols, tile_values):
    node_dev, width = features.shape
    _, block, _ = tile_values.shape
    blocks_dev = node_dev // block
    n = lax.axis_size("rows")
    ring = blocks_dev == 2 * n and n & (n - 1) == 0
    slots = max(n, blocks_dev * (1 if ring else HEAVY))
    blocks = features.reshape(blocks_dev, block, width)
    swap = functools.partial(lax.all_to_all, axis_name="rows", split_axis=0, concat_axis=0, tiled=True)
    tie = lax.optimization_barrier
    if ring:
        lists = 2 + 2 * n
        heavy_ids, mine, want, letters = start_up(n, blocks_dev, tile_cols, blocks)
        got = {}
        for m in (*range(n // 2, n), *range(1, n // 2)):
            got[m] = lax.ppermute(letters[m - 1], "rows", [(i, i ^ m) for i in range(n)])
        flip = lambda x, m: lax.ppermute(x, "rows", [(i, i ^ m) for i in range(n)])
        want = [want, flip(want, 1)]
        pair = want[0] + want[1]
        want = [pair] + [flip(pair, m) for m in range(2, n, 2)]

        def second_block(k, mine, *want):
            me = lax.axis_index("rows")
            asked = sum(matrix[k, me] for matrix in want)
            return jnp.where(mine[0] == 1, n + k, jnp.clip(asked, 0, blocks_dev - 1))

        picked = pick_blocks(second_block, n, (mine, *want), blocks, pltpu.VMEM, pltpu.HBM)
        second_part = swap(picked)
        order = ring_order(n)
        up = [(order[i], order[(i + 1) % n]) for i in range(n)]
        down = [(b, a) for a, b in up]
        share = functools.partial(pick_blocks, lambda k, ids: ids[k], HEAVY, (heavy_ids,), at=pl.ANY, to=pltpu.VMEM)
        start = take_share(n, 0, heavy_ids, blocks, [got[m] for m in range(1, n)])
        start, row_counts = tie((start, row_counts))
        plan = order_tiles(n, blocks_dev, lists, True, tile_cols, row_counts, heavy_ids)
        add = functools.partial(add_products, plan, blocks_dev=blocks_dev, slots=slots)

        def hop_on(way, x):
            return lax.ppermute(x, "rows", up if way == "up" else down)

        def add_now(ready, tiles, total):
            lists, panels = zip(*ready)
            total, tiles = add(tiles, lists, panels, total)
            return tiles, total

        ahead = hop_on("up", start)
        straight = hop_on("down", start)
        sums = add_now([(0, blocks), (2, start)], tile_values, None)
        sums = add_now([(4, ahead), (2 * n, straight)], *sums)
        back = mine_back = share(second_part)
        ready = [(1, second_part), (3, back)]
        ahead = hop_on("up", ahead)
        for hop in range(1, n - 1):
            if hop < n - 2:
                ready.append((4 + 2 * hop, ahead))
            else:
                ready.append((2 * n + 1, ahead))
            if hop < n - 3:
                ahead = hop_on("up", ahead)
            elif hop == n - 3:
                mine_back, ahead = tie((mine_back, ahead))
                ahead = hop_on("up", mine_back)
            back = hop_on("down", back)
            sums = add_now(ready, *sums)
            ready = [(3 + 2 * hop, back)]
        _, total = add_now(ready, *sums)
    else:
        heavy_ids, _, want = find_wants(n, blocks_dev, tile_cols)
        asked = swap(want.reshape(n, 1))[:, 0]
        plan = order_tiles(n, blocks_dev, 3, False, tile_cols, row_counts, heavy_ids)
        piece = node_dev // n
        light = swap(blocks[asked])
        scattered = swap(features.reshape(n, piece, width))[heavy_ids]
        heavy = lax.all_gather(scattered, "rows", axis=1, tiled=True).reshape(HEAVY * blocks_dev, block, width)
        total, _ = add_products(plan, tile_values, (0, 1, 2), (blocks, light, heavy), None, blocks_dev, slots)
    aggregate = total.reshape(node_dev, width)
    square_sum = jnp.sum(lax.all_gather(jnp.sum(aggregate * aggregate, axis=1), "feat"), axis=0)
    mean_square = square_sum / (width * lax.axis_size("feat"))
    return aggregate * norm_gain[None, :] * lax.rsqrt(mean_square + 1e-05)[:, None]


def solution(mesh):
    placed = (P("rows", "feat"), P("feat"), P("rows", None), P("rows"), P("rows", None, None))
    return jax.shard_map(per_device, mesh=mesh, in_specs=placed, out_specs=P("rows", "feat"), check_vma=False)
```

```python
import functools

import jax
import jax.numpy as jnp
from jax import lax
from jax.experimental import pallas as pl
from jax.experimental.pallas import tpu as pltpu
from jax.sharding import PartitionSpec as P


HEAVY = 3
SMEM = pl.BlockSpec(memory_space=pltpu.SMEM)
HBM = pl.BlockSpec(memory_space=pltpu.HBM)
ANY = pl.BlockSpec(memory_space=pl.ANY)
VMEM = pl.BlockSpec(memory_space=pltpu.VMEM)


def ring_order(n):
    return list(range(0, n, 2)) + list(range(n - 1, 0, -2))


def ring_place(index, n):
    return jnp.where(index % 2 == 0, index // 2, n - 1 - index // 2)


def find_heavy(n, blocks_dev, tile_total, cols_ref, heavy_ref, mine_ref, seen_ref, last_ref):
    me = lax.axis_index("rows")

    @pl.loop(0, n)
    def _(o):
        seen_ref[o] = 0
        last_ref[o] = 0

    @pl.loop(0, tile_total)
    def _(t):
        col = cols_ref[t]
        owner = col // blocks_dev
        seen_ref[owner] = seen_ref[owner] + 1
        last_ref[owner] = col % blocks_dev

    for k in range(HEAVY):
        heavy_ref[k] = 0

    def count(o, found):
        return found + ((seen_ref[o] >= 2) & (o != me)).astype(jnp.int32)

    others = lax.fori_loop(0, n, count, 0)
    mine = (others < HEAVY).astype(jnp.int32)
    mine_ref[0] = mine

    def rank(o, found):
        is_heavy = ((seen_ref[o] >= 2) & (o != me)) | ((o == me) & (mine == 1))

        @pl.when(is_heavy)
        def _():
            heavy_ref[jnp.minimum(found, HEAVY - 1)] = o

        return found + is_heavy.astype(jnp.int32)

    lax.fori_loop(0, n, rank, 0)


def wants_kernel(n, blocks_dev, tile_total, cols_ref, heavy_ref, mine_ref, want_ref, seen_ref):
    find_heavy(n, blocks_dev, tile_total, cols_ref, heavy_ref, mine_ref, seen_ref, want_ref)


def find_wants(n, blocks_dev, tile_cols):
    tile_total = tile_cols.shape[0]
    ints = lambda count: jax.ShapeDtypeStruct((count,), jnp.int32)
    return pl.pallas_call(
        functools.partial(wants_kernel, n, blocks_dev, tile_total),
        out_shape=(ints(HEAVY), ints(1), ints(n)),
        in_specs=[SMEM],
        out_specs=(SMEM,) * 3,
        scratch_shapes=[pltpu.SMEM((n,), jnp.int32)],
        name="wants",
    )(tile_cols)


def letters_kernel(n, from_ref, *refs):
    letters, sem_ref = refs[: n - 1], refs[n - 1]
    copies = [pltpu.make_async_copy(from_ref.at[m], letters[m - 1], sem_ref.at[m - 1]) for m in range(1, n)]
    for copy in copies:
        copy.start()
    for copy in copies:
        copy.wait()


def write_letters(n, blocks):
    return pl.pallas_call(
        functools.partial(letters_kernel, n),
        out_shape=[pltpu.VMEM(blocks.shape[1:], jnp.float32)] * (n - 1),
        in_specs=[HBM],
        out_specs=[VMEM] * (n - 1),
        scratch_shapes=[pltpu.SemaphoreType.DMA((n - 1,))],
        compiler_params=pltpu.CompilerParams(vmem_limit_bytes=58 << 20),
        name="letters",
    )(pltpu.with_memory_space_constraint(blocks, pltpu.HBM))


def asks_kernel(n, blocks_dev, tile_total, cols_ref, heavy_ref, mine_ref, want_ref, seen_ref, last_ref):
    me = lax.axis_index("rows")
    for o in range(n):
        for p in range(n):
            want_ref[o, p] = 0
    find_heavy(n, blocks_dev, tile_total, cols_ref, heavy_ref, mine_ref, seen_ref, last_ref)
    for p in range(n):
        want_ref[me, p] = last_ref[p]


def find_asks(n, blocks_dev, tile_cols):
    tile_total = tile_cols.shape[0]
    return pl.pallas_call(
        functools.partial(asks_kernel, n, blocks_dev, tile_total),
        out_shape=(
            jax.ShapeDtypeStruct((HEAVY,), jnp.int32),
            jax.ShapeDtypeStruct((1,), jnp.int32),
            jax.ShapeDtypeStruct((n, n), jnp.int32),
        ),
        in_specs=[SMEM],
        out_specs=(SMEM,) * 3,
        scratch_shapes=[pltpu.SMEM((n,), jnp.int32), pltpu.SMEM((n,), jnp.int32)],
        compiler_params=pltpu.CompilerParams(vmem_limit_bytes=8 << 20),
        name="asks",
    )(tile_cols)


def share_kernel(n, home, heavy_ref, from_ref, *refs):
    got, (out_ref, sem_ref) = refs[: n - 1], refs[n - 1:]
    me = lax.axis_index("rows")
    for k in range(HEAVY):
        away = heavy_ref[k] ^ me
        for m in range(n):
            source = from_ref.at[home] if m == 0 else got[m - 1]

            @pl.when(away == m)
            def _(source=source, k=k):
                pltpu.make_async_copy(source, out_ref.at[k], sem_ref.at[k]).start()

    for k in range(HEAVY):
        pltpu.make_async_copy(from_ref.at[home], out_ref.at[k], sem_ref.at[k]).wait()


def take_share(n, home, heavy_ids, blocks, got):
    _, block, width = blocks.shape
    return pl.pallas_call(
        functools.partial(share_kernel, n, home),
        out_shape=jax.ShapeDtypeStruct((HEAVY, block, width), jnp.float32),
        in_specs=[SMEM, ANY] + [ANY] * (n - 1),
        out_specs=VMEM,
        scratch_shapes=[pltpu.SemaphoreType.DMA((HEAVY,))],
        compiler_params=pltpu.CompilerParams(vmem_limit_bytes=8 << 20),
        cost_estimate=pl.CostEstimate(flops=0, bytes_accessed=8 * HEAVY * block * width, transcendentals=0),
        name="share",
    )(heavy_ids, blocks, *got)


def order_kernel(
    n, blocks_dev, tile_total, lists, ring, cols_ref, counts_ref, heavy_ref, plan_ref, list_ref, code_ref
):
    me = lax.axis_index("rows")
    here = ring_place(me, n)
    slots = max(n, blocks_dev * (1 if ring else HEAVY))

    @pl.loop(0, lists)
    def _(g):
        plan_ref[g] = 0

    def row_body(j, t0):
        def tile_body(t, carry):
            col = cols_ref[t]
            owner = col // blocks_dev
            local = col % blocks_dev
            heavy_at = jnp.int32(-1)
            for k in range(HEAVY):
                heavy_at = jnp.where(owner == heavy_ref[k], k, heavy_at)
            if ring:
                half = local // n
                there = ring_place(jnp.where(half == 0, owner ^ (local % n), local % n), n)
                hops = jnp.where(half == 0, here - there, there - here)
                hops = jnp.where(hops < 0, hops + n, hops)
                single = (half == 1) & (hops == n - 2) & (heavy_at == HEAVY - 1)
                heavy_list = jnp.where(single, 2 * n + 2, 2 + 2 * hops + half)
                heavy_slot = jnp.where(single, 0, heavy_at)
            else:
                heavy_list, heavy_slot = 2, heavy_at * blocks_dev + local
            own = owner == me
            which = jnp.where(own, 0, jnp.where(heavy_at < 0, 1, heavy_list))
            slot = jnp.where(own, local, jnp.where(heavy_at < 0, owner, heavy_slot))
            list_ref[t] = which
            plan_ref[which] = plan_ref[which] + 1
            code_ref[t] = (t * blocks_dev + j) * slots + slot
            return carry

        stop = jnp.minimum(t0 + counts_ref[0, j], tile_total)
        lax.fori_loop(t0, stop, tile_body, 0)
        return stop

    lax.fori_loop(0, counts_ref.shape[1], row_body, 0)

    def add_up(g, total):
        count = plan_ref[g]
        plan_ref[g] = total
        return total + count

    lax.fori_loop(0, lists, add_up, 0)

    @pl.loop(0, tile_total)
    def _(t):
        which = list_ref[t]
        at = plan_ref[which]
        plan_ref[which] = at + 1
        plan_ref[lists + at] = code_ref[t]


def order_tiles(n, blocks_dev, lists, ring, tile_cols, row_counts, heavy_ids):
    tile_total = tile_cols.shape[0]
    return pl.pallas_call(
        functools.partial(order_kernel, n, blocks_dev, tile_total, lists, ring),
        out_shape=jax.ShapeDtypeStruct((lists + tile_total,), jnp.int32),
        in_specs=[SMEM] * 3,
        out_specs=SMEM,
        scratch_shapes=[pltpu.SMEM((tile_total,), jnp.int32), pltpu.SMEM((tile_total,), jnp.int32)],
        name="order",
    )(tile_cols, row_counts, heavy_ids)


def pick_kernel(choose, count, *refs):
    index_refs, from_ref, out_ref, sem_ref = refs[:-3], refs[-3], refs[-2], refs[-1]
    copies = [
        pltpu.make_async_copy(from_ref.at[choose(k, *index_refs)], out_ref.at[k], sem_ref.at[k])
        for k in range(count)
    ]
    for copy in copies:
        copy.start()
    for copy in copies:
        copy.wait()


def pick_blocks(choose, count, indices, blocks, at, to):
    return pl.pallas_call(
        functools.partial(pick_kernel, choose, count),
        out_shape=to((count, *blocks.shape[1:]), blocks.dtype),
        in_specs=[SMEM] * len(indices) + [pl.BlockSpec(memory_space=at)],
        out_specs=pl.BlockSpec(memory_space=to),
        scratch_shapes=[pltpu.SemaphoreType.DMA((count,))],
        compiler_params=pltpu.CompilerParams(vmem_limit_bytes=8 << 20),
        cost_estimate=pl.CostEstimate(
            flops=0, bytes_accessed=8 * count * blocks.shape[1] * blocks.shape[2], transcendentals=0
        ),
        name="pick",
    )(*indices, blocks)


def halves(x):
    high = x.astype(jnp.bfloat16)
    low = (x - high.astype(jnp.float32)).astype(jnp.bfloat16)
    return high, low


def add_kernel(lists, all_lists, slots, first, plan_ref, tiles_ref, *refs):
    panels = refs[: len(lists)]
    if first:
        out_ref, kept_ref, sem_ref = refs[len(lists):]
        bring = pltpu.make_async_copy(tiles_ref, kept_ref, sem_ref)
        bring.start()
        out_ref[...] = jnp.zeros_like(out_ref)
        bring.wait()
        tiles_ref = kept_ref
    else:
        out_ref = refs[-1]
    blocks_dev = out_ref.shape[0]
    for which, panel in zip(lists, panels):
        begin = plan_ref[which - 1] if which else 0

        @pl.loop(begin, plan_ref[which])
        def _(i):
            code = plan_ref[all_lists + i]
            at, slot = code // slots, code % slots
            tile, row = at // blocks_dev, at % blocks_dev
            a_high, a_low = halves(tiles_ref[tile])
            x_high, x_low = halves(jnp.maximum(panel[slot], 0.0))
            left = jnp.concatenate([a_high, a_low, a_high], axis=1)
            right = jnp.concatenate([x_high, x_high, x_low], axis=0)
            out_ref[row] += jnp.dot(left, right, preferred_element_type=jnp.float32)


def add_products(plan, tiles, lists, panels, into, blocks_dev, slots):
    tile_total, block, _ = tiles.shape
    width = panels[0].shape[-1]
    first = into is None
    operands = [plan, tiles, *panels] + ([] if first else [into])
    total = pltpu.VMEM((blocks_dev, block, width), jnp.float32)
    done = pl.pallas_call(
        functools.partial(add_kernel, lists, plan.shape[0] - tile_total, slots, first),
        out_shape=(total, pltpu.VMEM(tiles.shape, tiles.dtype)) if first else total,
        in_specs=[SMEM, HBM if first else VMEM] + [VMEM] * (len(operands) - 2),
        out_specs=(VMEM, VMEM) if first else VMEM,
        scratch_shapes=[pltpu.SemaphoreType.DMA] if first else [],
        input_output_aliases={} if first else {len(operands) - 1: 0},
        compiler_params=pltpu.CompilerParams(vmem_limit_bytes=16 << 20),
        cost_estimate=pl.CostEstimate(
            flops=20 * len(lists) * block * block * width,
            bytes_accessed=4 * blocks_dev * block * width,
            transcendentals=0,
        ),
        name="add",
    )(*operands)
    return done if first else (done, tiles)


def per_device(features, norm_gain, row_counts, tile_cols, tile_values):
    node_dev, width = features.shape
    _, block, _ = tile_values.shape
    blocks_dev = node_dev // block
    n = lax.axis_size("rows")
    ring = blocks_dev == 2 * n and n & (n - 1) == 0
    slots = max(n, blocks_dev * (1 if ring else HEAVY))
    blocks = features.reshape(blocks_dev, block, width)
    swap = functools.partial(lax.all_to_all, axis_name="rows", split_axis=0, concat_axis=0, tiled=True)
    tie = lax.optimization_barrier
    if ring:
        lists = 3 + 2 * n
        letters = write_letters(n, blocks)
        got = {}
        for m in (*range(n // 2, n), *range(1, n // 2)):
            got[m] = lax.ppermute(letters[m - 1], "rows", [(i, i ^ m) for i in range(n)])
        heavy_ids, mine, want = find_asks(n, blocks_dev, tile_cols)
        flip = lambda x, m: lax.ppermute(x, "rows", [(i, i ^ m) for i in range(n)])
        want = [want, flip(want, 1)]
        pair = want[0] + want[1]
        want = [pair] + [flip(pair, m) for m in range(2, n, 2)]

        def second_block(k, mine, *want):
            me = lax.axis_index("rows")
            asked = sum(matrix[k, me] for matrix in want)
            return jnp.where(mine[0] == 1, n + k, jnp.clip(asked, 0, blocks_dev - 1))

        picked = pick_blocks(second_block, n, (mine, *want), blocks, pltpu.VMEM, pltpu.HBM)
        second_part = swap(picked)
        order = ring_order(n)
        up = [(order[i], order[(i + 1) % n]) for i in range(n)]
        down = [(b, a) for a, b in up]
        share = functools.partial(pick_blocks, lambda k, ids: ids[k], HEAVY, (heavy_ids,), at=pl.ANY, to=pltpu.VMEM)
        start = take_share(n, 0, heavy_ids, blocks, [got[m] for m in range(1, n)])
        start, row_counts = tie((start, row_counts))
        plan = order_tiles(n, blocks_dev, lists, True, tile_cols, row_counts, heavy_ids)
        add = functools.partial(add_products, plan, blocks_dev=blocks_dev, slots=slots)

        def hop_on(way, x):
            return lax.ppermute(x, "rows", up if way == "up" else down)

        def add_now(ready, tiles, total):
            lists, panels = zip(*ready)
            total, tiles = add(tiles, lists, panels, total)
            return tiles, total

        ahead = hop_on("up", start)
        straight = hop_on("down", start)
        sums = add_now([(0, blocks), (2, start)], tile_values, None)
        sums = add_now([(4, ahead), (2 * n, straight)], *sums)
        back = mine_back = share(second_part)
        ready = [(1, second_part), (3, back)]
        ahead = hop_on("up", ahead)
        for hop in range(1, n - 1):
            if hop < n - 2:
                ready.append((4 + 2 * hop, ahead))
            else:
                ready.append((2 * n + 1, ahead))
            if hop < n - 3:
                ahead = hop_on("up", ahead)
            elif hop == n - 3:
                mine_back, ahead = tie((mine_back, ahead))
                ahead = hop_on("up", mine_back)
            if hop < n - 2:
                back = hop_on("down", back)
            else:
                last = hop_on("up", ahead[HEAVY - 1:])
                back = hop_on("down", back[: HEAVY - 1])
            sums = add_now(ready, *sums)
            ready = [(3 + 2 * hop, back)]
        _, total = add_now([*ready, (2 * n + 2, last)], *sums)
    else:
        heavy_ids, _, want = find_wants(n, blocks_dev, tile_cols)
        asked = swap(want.reshape(n, 1))[:, 0]
        plan = order_tiles(n, blocks_dev, 3, False, tile_cols, row_counts, heavy_ids)
        piece = node_dev // n
        light = swap(blocks[asked])
        scattered = swap(features.reshape(n, piece, width))[heavy_ids]
        heavy = lax.all_gather(scattered, "rows", axis=1, tiled=True).reshape(HEAVY * blocks_dev, block, width)
        total, _ = add_products(plan, tile_values, (0, 1, 2), (blocks, light, heavy), None, blocks_dev, slots)
    aggregate = total.reshape(node_dev, width)
    squares = jnp.sum(aggregate * aggregate, axis=1)
    parts = lax.axis_size("feat")
    square_sum = squares
    for shift in range(1, parts):
        square_sum += lax.ppermute(squares, "feat", [(i, (i + shift) % parts) for i in range(parts)])
    mean_square = square_sum / (width * lax.axis_size("feat"))
    return aggregate * norm_gain[None, :] * lax.rsqrt(mean_square + 1e-05)[:, None]


def solution(mesh):
    placed = (P("rows", "feat"), P("feat"), P("rows", None), P("rows"), P("rows", None, None))
    return jax.shard_map(per_device, mesh=mesh, in_specs=placed, out_specs=P("rows", "feat"), check_vma=False)
```
